256 devices in a mesh: row: 16 (over x_hi, y, core), col: 16 (over x_lo, z).
Axes of the slice: x: 4 (x_hi: 2, x_lo: 2; x = x_hi * 2 + x_lo), y: 4, z: 8, core: 2. Of those that a mesh axis runs over, the one named last changes fastest.
Arguments:
- slab: float32 [24576, 24576], P('row', 'col'), may hold values from -0.0546875 to 0.0546875
- amps: float32 [24576, 768], P(('row', 'col')), may hold values from -6 to 6
- drive_first: float32 [24576, 768], P(('col', 'row')), may hold values from -6 to 6
- drive_second: float32 [24576, 768], P(('row', 'col')), may hold values from -6 to 6
- vir_pairs: int32 [2, 24576], replicated, may hold values from 0 to 159
- occ_pairs: int32 [2, 768], replicated, may hold values from 0 to 63
- e_vir: float32 [160], replicated, may hold values from 0.3 to 3
- e_occ: float32 [64], replicated, may hold values from -3 to -0.3
Outputs:
- amps_second: float32 [24576, 768], P(('row', 'col'))
The draws below stay inside these ranges and needn't reach their ends.
All inputs are finite; a program needn't handle non-finite values.
Results may differ from the reference program's by a relative error of at most 0.00005.
Values sent between devices are 32-bit elements; how exact they have to be, the bound alone decides.
No kernel may reach another device: no remote copies, remote signals or barrier semaphores. Data moves between devices by JAX's collectives and lax.ppermute only.
A program may use at most 64 MiB of HBM per device.

```python
import jax
import jax.numpy as jnp
from jax import lax

NV2 = 24576
NVIR = 160
NOCC = 64
NP = 768


def touch_ends(entries, stream_key, low, top_value):
    spot = [jax.random.randint(jax.random.fold_in(stream_key, axis), (), 0, length) for axis, length in enumerate(entries.shape)]
    main_axis = entries.shape.index(max(entries.shape))
    beside = spot[:main_axis] + [(spot[main_axis] + 1) % entries.shape[main_axis]] + spot[main_axis + 1:]
    return entries.at[tuple(spot)].set(low).at[tuple(beside)].set(top_value)


def with_spikes(entries, stream_key, source, target, parts, factor):
    def block_of(dim):
        return (jnp.arange(entries.shape[dim]) // (entries.shape[dim] // parts)).reshape((-1,) + (1,) * (entries.ndim - 1 - dim))

    near = jax.random.permutation(stream_key, parts)[block_of(target)]
    other_side = (block_of(target) + parts // 2) % parts
    return jnp.where((block_of(source) == near) | (block_of(source) == other_side), factor * entries, entries)


def level_of(stream_key, shape, split, low, high):
    loudness, own = 1.0, jax.random.fold_in(stream_key, 6)
    for dim, shards_of in split:
        steps = jnp.exp(jax.random.uniform(jax.random.fold_in(own, dim), (shards_of,), jnp.float32, low / len(split), high / len(split)))
        loudness = loudness * jnp.repeat(steps, shape[dim] // shards_of).reshape([-1 if axis == dim else 1 for axis in range(len(shape))])
    return loudness


def bell_draw(rng, dims, width, bound, split=(), held_as=jnp.bfloat16):
    array = jax.random.normal(rng, dims, jnp.float32) * width
    if len(split) > 0:
        array = level_of(rng, dims, split, -0.22, 0.18) * array
    return jnp.clip(array, min=-bound, max=bound).astype(held_as)


def gaussian_with(stream_key, extent, width, reach, split, heavy, held_as=jnp.bfloat16):
    result = width * jax.random.normal(stream_key, extent, jnp.float32)
    if split:
        result = result * level_of(stream_key, extent, split, -0.22, 0.18)
    return jnp.clip(with_spikes(result, jax.random.fold_in(stream_key, 3), *heavy), -reach, reach).astype(held_as)


def setup_inputs(seed: int = 0) -> dict:
    keys = jax.random.split(jax.random.key(seed), 9)
    slab = gaussian_with(keys[0], (NV2, NV2), NV2 ** -0.5, 0.0546875, ((0, 16), (1, 16)), (0, 1, 16, 2.0), jnp.float32)
    amps = bell_draw(keys[1], (NV2, NP), 1.0, 6.0, ((0, 256),), jnp.float32)
    drive_first = bell_draw(keys[2], (NV2, NP), 1.0, 6.0, ((0, 256),), jnp.float32)
    drive_second = bell_draw(keys[3], (NV2, NP), 1.0, 6.0, ((0, 256),), jnp.float32)
    vir_pairs = touch_ends(jax.random.randint(keys[4], (2, NV2), 0, NVIR), jax.random.fold_in(keys[4], 1), 0, NVIR - 1).astype(jnp.int32)
    occ_pairs = touch_ends(jax.random.randint(keys[5], (2, NP), 0, NOCC), jax.random.fold_in(keys[5], 1), 0, NOCC - 1).astype(jnp.int32)
    e_vir = jnp.clip(jax.random.uniform(keys[6], (NVIR,), jnp.float32, 0.3, 3.0), 0.3, 3.0)
    e_occ = jnp.clip(jax.random.uniform(keys[7], (NOCC,), jnp.float32, -3.0, -0.3), -3.0, -0.3)
    return dict(slab=slab, amps=amps, drive_first=drive_first, drive_second=drive_second, vir_pairs=vir_pairs, occ_pairs=occ_pairs, e_vir=e_vir, e_occ=e_occ)


def orbital_gaps(vir_pairs, occ_pairs, e_vir, e_occ):
    virtual = e_vir[vir_pairs[0]] + e_vir[vir_pairs[1]]
    occupied = e_occ[occ_pairs[0]] + e_occ[occ_pairs[1]]
    return virtual[:, None] - occupied[None, :]


def reference(slab, amps, drive_first, drive_second, vir_pairs, occ_pairs, e_vir, e_occ):
    gap_table = orbital_gaps(vir_pairs, occ_pairs, e_vir, e_occ)
    first = lax.dot_general(slab, amps, (((0,), (0,)), ((), ())), precision=lax.Precision.HIGHEST, preferred_element_type=jnp.float32)
    amps_first = (drive_first + first) / gap_table
    second = jnp.dot(slab, amps_first, precision=lax.Precision.HIGHEST, preferred_element_type=jnp.float32)
    return (drive_second + second) / gap_table
```

```python
import jax
import jax.numpy as jnp
from jax import lax
from jax.experimental import pallas as pl
from jax.experimental.pallas import tpu as pltpu
from jax.sharding import PartitionSpec as P


XH, Y, CORE, XL, Z = 2, 4, 2, 2, 8
SHARD = 96
NV = 1536
AXES = ("row", "col")
bf16, f32 = jnp.bfloat16, jnp.float32


def permutation(move):
    pairs = []
    for xh in range(XH):
        for y in range(Y):
            for core in range(CORE):
                for xl in range(XL):
                    for z in range(Z):
                        a = (((xh * Y + y) * CORE + core) * XL + xl) * Z + z
                        h, v, k, l, w = move(xh, y, core, xl, z)
                        b = (((h * Y + v % Y) * CORE + k) * XL + l) * Z + w % Z
                        pairs.append((a, b))
    return pairs


def z_shift(d):
    return permutation(lambda xh, y, core, xl, z: (xh, y, core, xl, z + d))


X_PAIR = permutation(lambda xh, y, core, xl, z: (xh, y, core, 1 - xl, z))
CORE_PAIR = permutation(lambda xh, y, core, xl, z: (xh, y, 1 - core, xl, z))
UP, DOWN = z_shift(1), z_shift(-1)


def chip_shift(dxh, dy):
    return permutation(lambda xh, y, core, xl, z: (xh ^ dxh, y + dy, core, xl, z))


def send(value, pairs):
    return lax.ppermute(value, AXES, pairs)


def row_position():
    row = lax.axis_index("row")
    return row // (Y * CORE), (row // CORE) % Y, row % CORE


def col_position():
    col = lax.axis_index("col")
    return col // Z, col % Z


def row_block(dxh, dy, dcore):
    xh, y, core = row_position()
    return (((xh + dxh) % XH) * Y + (y + dy + Y) % Y) * CORE + (core + dcore) % CORE


def col_block(dxl, dz):
    xl, z = col_position()
    return ((xl + dxl) % XL) * Z + (z + dz + Z) % Z


def rows_at(block, count=SHARD):
    return pl.ds(pl.multiple_of(block * SHARD, SHARD), count)


def split(value):
    high = value.astype(bf16)
    return high, (value - high.astype(f32)).astype(bf16)


def prepare_kernel(slab_ref, high_ref, low_ref):
    step = pl.program_id(0)
    for part in range(4):
        block = step * 4 + part
        xl, z = col_position()
        dxl = (block // Z - xl + XL) % XL
        dz = (block % Z - z + Z) % Z
        high, low = split(slab_ref[part * SHARD : (part + 1) * SHARD, :])
        high_ref[rows_at(dxl * Z + dz), :] = high
        low_ref[rows_at(dxl * Z + dz), :] = low


def prepare_transposed_kernel(slab_ref, high_ref, low_ref):
    step = pl.program_id(0)
    xh, y, core = row_position()
    depth = 256
    for k in range(NV // depth):
        turned = slab_ref[k * depth : (k + 1) * depth, :].T
        for part in range(4):
            block = step * 4 + part
            dxh = (block // (Y * CORE) - xh + XH) % XH
            dy = ((block // CORE) % Y - y + Y) % Y
            dcore = (block % CORE - core + CORE) % CORE
            high, low = split(turned[part * SHARD : (part + 1) * SHARD, :])
            target = rows_at((dcore * XH + dxh) * Y + dy)
            high_ref[target, k * depth : (k + 1) * depth] = high
            low_ref[target, k * depth : (k + 1) * depth] = low


def prepare(slab, transposed):
    wide = 4 * SHARD
    in_block = pl.BlockSpec((NV, wide), lambda i: (0, i)) if transposed else pl.BlockSpec((wide, NV), lambda i: (i, 0))
    whole = pl.BlockSpec((NV, NV), lambda i: (0, 0), pipeline_mode=pl.Buffered(1))
    return pl.pallas_call(
        prepare_transposed_kernel if transposed else prepare_kernel,
        grid=(NV // wide,),
        in_specs=[in_block],
        out_specs=[whole, whole],
        out_shape=[jax.ShapeDtypeStruct((NV, NV), bf16)] * 2,
        cost_estimate=pl.CostEstimate(flops=NV * NV * 4, bytes_accessed=NV * NV * 8, transcendentals=0),
        compiler_params=pltpu.CompilerParams(vmem_limit_bytes=24 << 20),
        name="prepare_t" if transposed else "prepare",
    )(slab)


def product(high, low, pieces, places, width, row_start, row_count):
    tile = 384

    def kernel(high_ref, low_ref, *refs):
        piece_refs, out_ref, a_high, a_low = refs[: len(pieces)], refs[-3], refs[-2], refs[-1]

        @pl.when(pl.program_id(0) == 0)
        def _():
            for ref, place in zip(piece_refs, places):
                for block, row, column in place():
                    h, l = split(ref[row : row + SHARD, :])
                    cols = pl.ds(column, ref.shape[1])
                    a_high[rows_at(block), cols] = h
                    a_low[rows_at(block), cols] = l

        total = jnp.dot(high_ref[...], a_low[...], preferred_element_type=f32)
        total += jnp.dot(low_ref[...], a_high[...], preferred_element_type=f32)
        total += jnp.dot(high_ref[...], a_high[...], preferred_element_type=f32)
        out_ref[...] = total

    slab_block = pl.BlockSpec((tile, NV), lambda i: (i + row_start // tile, 0))
    return pl.pallas_call(
        kernel,
        grid=(row_count // tile,),
        in_specs=[slab_block, slab_block]
        + [pl.BlockSpec(p.shape, lambda i: (0, 0), pipeline_mode=pl.Buffered(1)) for p in pieces],
        out_specs=pl.BlockSpec((tile, width), lambda i: (i, 0)),
        out_shape=jax.ShapeDtypeStruct((row_count, width), f32),
        scratch_shapes=[pltpu.VMEM((NV, width), bf16)] * 2,
        cost_estimate=pl.CostEstimate(
            flops=6 * row_count * NV * width, bytes_accessed=row_count * NV * 4 + NV * width * 4, transcendentals=0
        ),
        compiler_params=pltpu.CompilerParams(vmem_limit_bytes=28 << 20),
        name="product",
    )(high, low, *pieces)


def gather_col_x_first(own):
    pair = jnp.concatenate([own, send(own, X_PAIR)], axis=0)
    pieces, places = [pair], [lambda: [(col_block(0, 0), 0, 0), (col_block(1, 0), SHARD, 0)]]
    up = down = pair
    for d in range(1, 4):
        up, down = send(up, UP), send(down, DOWN)
        pieces += [up, down]
        places += [
            lambda d=d: [(col_block(0, -d), 0, 0), (col_block(1, -d), SHARD, 0)],
            lambda d=d: [(col_block(0, d), 0, 0), (col_block(1, d), SHARD, 0)],
        ]
    pieces += [send(up[:SHARD], UP), send(down[SHARD:], DOWN)]
    places += [lambda: [(col_block(0, 4), 0, 0)], lambda: [(col_block(1, 4), 0, 0)]]
    return pieces, places


def gather_col_z_first(own):
    half = own.shape[1] // 2
    pieces, places = [own], [lambda: [(col_block(0, 0), 0, 0)]]
    across = send(own, X_PAIR)
    pieces.append(across)
    places.append(lambda: [(col_block(1, 0), 0, 0)])
    up = down = own
    for d in range(1, 4):
        up, down = send(up, UP), send(down, DOWN)
        across = send(jnp.concatenate([up, down], axis=0), X_PAIR)
        pieces += [up, down, across]
        places += [
            lambda d=d: [(col_block(0, -d), 0, 0)],
            lambda d=d: [(col_block(0, d), 0, 0)],
            lambda d=d: [(col_block(1, -d), 0, 0), (col_block(1, d), SHARD, 0)],
        ]
    far = jnp.concatenate([send(up[:, :half], UP), send(down[:, half:], DOWN)], axis=1)
    pieces += [far, send(far, X_PAIR)]
    places += [lambda: [(col_block(0, 4), 0, 0)], lambda: [(col_block(1, 4), 0, 0)]]
    return pieces, places


def reduce_col_z_first(partial):
    def pair(dz):
        dz %= Z
        return jnp.concatenate([partial[dz * SHARD : (dz + 1) * SHARD], partial[(Z + dz) * SHARD : (Z + dz + 1) * SHARD]], axis=0)

    far = pair(4)
    up, down = send(far[:SHARD], UP), send(far[SHARD:], DOWN)
    zero = jnp.zeros_like(up)
    up, down = jnp.concatenate([up, zero], axis=0), jnp.concatenate([zero, down], axis=0)
    for d in (3, 2, 1):
        up, down = send(pair(d) + up, UP), send(pair(-d) + down, DOWN)
    total = pair(0) + up + down
    return total[:SHARD] + send(total[SHARD:], X_PAIR)


def reduce_col_x_first(partial):
    half = partial.shape[1] // 2

    def block(dxl, dz):
        start = (dxl * Z + dz % Z) * SHARD
        return partial[start : start + SHARD]

    def joined(d):
        got = send(jnp.concatenate([block(1, d), block(1, -d)], axis=0), X_PAIR)
        return block(0, d) + got[:SHARD], block(0, -d) + got[SHARD:]

    far = block(0, 4) + send(block(1, 4), X_PAIR)
    up, down = send(far[:, :half], UP), send(far[:, half:], DOWN)
    zero = jnp.zeros_like(up)
    up, down = jnp.concatenate([up, zero], axis=1), jnp.concatenate([zero, down], axis=1)
    for d in (3, 2, 1):
        ahead, behind = joined(d)
        up, down = send(ahead + up, UP), send(behind + down, DOWN)
    return block(0, 0) + send(block(1, 0), X_PAIR) + up + down


OTHERS = [(0, 1), (0, 3), (1, 0), (1, 1), (1, 3), (0, 2), (1, 2)]


def reduce_row(mine, others):
    got = send(others, CORE_PAIR)

    def block(dxh, dy):
        start = (dxh * Y + dy) * SHARD
        return mine[start : start + SHARD] + got[start : start + SHARD]

    return [send(block(dxh, dy), chip_shift(dxh, dy)) for dxh, dy in OTHERS] + [block(0, 0)]


def gather_row(own):
    pieces = [own] + [send(own, chip_shift(dxh, dy)) for dxh, dy in OTHERS]
    other = send(jnp.concatenate(pieces, axis=0), CORE_PAIR)
    sources = [(0, 0)] + [(dxh, -dy) for dxh, dy in OTHERS]
    places = [lambda s=s: [(row_block(s[0], s[1], 0), 0, 0)] for s in sources]
    places.append(lambda: [(row_block(s[0], s[1], 1), i * SHARD, 0) for i, s in enumerate(sources)])
    return pieces + [other], places


def lookup(index_table, energies):
    levels = lax.broadcasted_iota(
        jnp.int32, index_table.shape + (energies.shape[0],), index_table.ndim
    )
    return jnp.sum(jnp.where(index_table[..., None] == levels, energies, jnp.float32(0.0)), axis=-1)


def local(slab, amps, drive_first, drive_second, vir_pairs, occ_pairs, e_vir, e_occ):
    shard_rows = amps.shape[0]
    row_count = lax.axis_size("row")
    col_count = lax.axis_size("col")
    row_index = lax.axis_index("row")
    col_index = lax.axis_index("col")
    first_offset = (col_index * row_count + row_index) * shard_rows
    second_offset = (row_index * col_count + col_index) * shard_rows
    occupied = lookup(occ_pairs[0], e_occ) + lookup(occ_pairs[1], e_occ)

    def virtual(offset):
        rows = lax.dynamic_slice_in_dim(vir_pairs, offset, shard_rows, 1)
        return lookup(rows[0], e_vir) + lookup(rows[1], e_vir)

    vir_first, vir_second = virtual(first_offset), virtual(second_offset)
    t_high, t_low = prepare(slab, True)
    high, low = prepare(slab, False)
    chunks = ((0, 256, True), (256, 512, False))
    results = []
    for start, width, x_first in chunks:
        cols = slice(start, start + width)
        gather = gather_col_x_first if x_first else gather_col_z_first
        reduce = reduce_col_z_first if x_first else reduce_col_x_first
        pieces, places = gather(amps[:, cols])
        others = product(t_high, t_low, pieces, places, width, NV // 2, NV // 2)
        mine = product(t_high, t_low, pieces, places, width, 0, NV // 2)
        terms = reduce_row(mine, others)
        gap_first = vir_first[:, None] - occupied[None, cols]
        first = (drive_first[:, cols] + sum(terms[1:], terms[0])) / gap_first
        pieces, places = gather_row(first)
        partial = product(high, low, pieces, places, width, 0, NV)
        gap_second = vir_second[:, None] - occupied[None, cols]
        results.append((drive_second[:, cols] + reduce(partial)) / gap_second)
    return jnp.concatenate(results, axis=1)


def solution(mesh):
    placed = (
        P("row", "col"),
        P(("row", "col"), None),
        P(("col", "row"), None),
        P(("row", "col"), None),
        P(),
        P(),
        P(),
        P(),
    )
    return jax.shard_map(
        local, mesh=mesh, in_specs=placed, out_specs=P(("row", "col"), None), check_vma=False
    )
```
